32 devices in a mesh: dp: 2 (over core), context: 4 (over y, x), tensor: 4 (over z).
Axes of the slice: x: 2, y: 2, z: 4, core: 2. Of those that a mesh axis runs over, the one named last changes fastest.
Arguments:
- hidden: bfloat16 [2, 1024, 8192], P('dp', 'context'), may hold values from -6 to 6
- inputs: bfloat16 [2, 1024, 8192], P('dp', 'context', 'tensor'), may hold values from -6 to 6
- upstream: bfloat16 [2, 1024, 8192], P('dp', 'context', 'tensor'), may hold values from -0.059814453 to 0.059814453
- proj_weight: bfloat16 [2048, 8192], P('tensor', ('dp', 'context')), may hold values from -0.0625 to 0.0625
- delta_weight: bfloat16 [128, 8192], P('tensor', ('dp', 'context')), may hold values from -0.0625 to 0.0625
- decay_rate: float32 [128], P('tensor'), may hold values from 9.765625e-05 to 0.125
- step_bias: float32 [128], P('tensor'), may hold values from -3 to 0
- proj_moment: float32 [2048, 8192], P('tensor', ('dp', 'context')), may hold values from -0.2 to 0.2
- proj_second: float32 [2048, 8192], P('tensor', ('dp', 'context')), may hold values from 0.0001 to 0.01
- delta_moment: float32 [128, 8192], P('tensor', ('dp', 'context')), may hold values from -0.2 to 0.2
- delta_second: float32 [128, 8192], P('tensor', ('dp', 'context')), may hold values from 0.0001 to 0.01
- doc_lengths: int32 [2, 4], P('dp'), may hold values from 1 to 512, 1024 in all within a row
- valid_counts: int32 [2, 4], P('dp', 'context'), may hold values from 64 to 256, as said below
Outputs:
- input_grad: bfloat16 [2, 1024, 8192], P('dp', 'context', 'tensor')
- hidden_grad: bfloat16 [2, 1024, 8192], P('dp', 'context', 'tensor')
- rate_grad: float32 [128], P('tensor')
- bias_grad: float32 [128], P('tensor')
- proj_update: float32 [2048, 8192], P('tensor', ('dp', 'context'))
- delta_update: float32 [128, 8192], P('tensor', ('dp', 'context'))
The draws below stay inside these ranges and needn't reach their ends.
Inputs may be any that keep to these rules, and one draw needn't show every extreme that they name: `doc_lengths`: the 4 lengths of a row sum to 1024, and the longest is exactly half of 1024. The first valid_counts[b, j] tokens of block j of row b are real, the rest padding; in every draw some block is full and another holds exactly 64.
All inputs are finite; a program needn't handle non-finite values.
Results may differ from the reference program's by a relative error of at most 0.014.
Values may be sent and summed in bfloat16 or wider, within the bound.
No kernel may reach another device: no remote copies, remote signals or barrier semaphores. Data moves between devices by JAX's collectives and lax.ppermute only.
A program may use at most 128 MiB of HBM per device.

```python
import math
import jax
import jax.numpy as jnp
import numpy as np
from jax import lax

D = 8192
H = 128
HEAD_DIM = 64
N = 256
G = 4
Q = 128
NDOC = 4
TOK_DEV = 256
SEQ = 1024
BATCH = 2
BLOCKS = 4
N_TENSOR = 4


def draw_valid_counts(key, part):
    first = jax.random.fold_in(key, 11)
    second = jax.random.fold_in(key, 23)
    counts = jax.random.randint(first, (BATCH * BLOCKS,), TOK_DEV // 4, TOK_DEV + 1, dtype=jnp.int32)
    spot = jax.random.randint(second, (), 0, BATCH * BLOCKS, dtype=jnp.int32)
    places = jnp.arange(BATCH * BLOCKS, dtype=jnp.int32)
    counts = jnp.where(places == spot, TOK_DEV, counts)
    counts = jnp.where(places == (spot + 1) % (BATCH * BLOCKS), TOK_DEV // 4, counts)
    return counts.reshape(BATCH, BLOCKS).astype(jnp.int32)


def block_levels(stream_key, shape, split, smallest, top_value):
    gain = 1.0
    for position, parts in split:
        heights = jax.random.uniform(jax.random.fold_in(jax.random.fold_in(stream_key, 6), position), (parts,), jnp.float32, smallest / len(split), top_value / len(split))
        gain = gain * jnp.repeat(jnp.exp(heights), shape[position] // parts).reshape((-1,) + (1,) * (len(shape) - 1 - position))
    return gain


def length_profile(count, total, bound, skew):
    weights = [(1 << 20) // math.isqrt(standing ** skew) + 1 for standing in range(2, count + 1)]
    rest, given = total - bound - (count - 1), [1] * (count - 1)
    while rest > 0:
        movable = [i for i in range(count - 1) if given[i] < bound]
        pool, budget = sum([weights[i] for i in movable]), rest
        for i in movable:
            addition = min(bound - given[i], max(1, budget * weights[i] // pool), rest)
            given[i] = given[i] + addition
            rest = rest - addition
    return np.array([bound] + given)


def ragged(stream_key, count, total, most, lean):
    if count == 2:
        one = jax.random.randint(stream_key, (), max(1, total - most), min(most, total - 1) + 1)
        return jnp.stack([one, total - one])
    sizes = jnp.asarray(length_profile(count, total, most, lean), jnp.int32)
    couples = (count - 1) // 2
    source_of, receiver = sizes[1:1 + 2 * couples:2], sizes[2:2 + 2 * couples:2]
    room = jnp.minimum(source_of - 1, most - receiver)
    shifted = jax.random.randint(jax.random.fold_in(stream_key, 1), (couples,), 0, 1 << 20) % (room + 1)
    sizes = sizes.at[1:1 + 2 * couples:2].set(source_of - shifted).at[2:2 + 2 * couples:2].set(receiver + shifted)
    return sizes[jax.random.permutation(jax.random.fold_in(stream_key, 2), count)]


def normal_values(stream_key, shape, scale, most, cuts=(), kind=jnp.bfloat16):
    loudness = block_levels(stream_key, shape, cuts, -0.22, 0.18) if cuts else 1.0
    values = jax.random.normal(stream_key, shape, jnp.float32) * scale * loudness
    return jnp.minimum(jnp.maximum(values, -most), most).astype(kind)


def setup_inputs(seed: int = 0) -> dict:
    keys = jax.random.split(jax.random.key(seed), 14)
    return {
        "hidden": normal_values(keys[0], (BATCH, SEQ, D), 1.0, 6.0, ((0, 2), (1, 4))),
        "inputs": normal_values(keys[1], (BATCH, SEQ, H * HEAD_DIM), 1.0, 6.0, ((0, 2), (1, 4), (2, 4))),
        "upstream": normal_values(keys[2], (BATCH, SEQ, H * HEAD_DIM), 0.01, 0.059814453, ((0, 2), (1, 4), (2, 4))),
        "proj_weight": normal_values(keys[3], (2 * G * N, D), D ** -0.5, 0.0625, ((0, 4), (1, 8))),
        "delta_weight": normal_values(keys[4], (H, D), D ** -0.5, 0.0625, ((0, 4), (1, 8))),
        "decay_rate": jnp.clip(jnp.exp(math.log(0.125) - 7.1546153 * jax.random.uniform(keys[5], (H,), jnp.float32) ** block_levels(keys[5], (H,), ((0, 4),), -0.2, 0.2)), 9.765625145519152e-05, 0.125),
        "step_bias": jnp.clip(-3.0 + 3.0 * jax.random.uniform(keys[6], (H,), jnp.float32) ** block_levels(keys[6], (H,), ((0, 4),), -0.2, 0.2), -3.0, 0.0),
        "proj_moment": normal_values(keys[7], (2 * G * N, D), 0.03, 0.2, ((0, 4), (1, 8)), jnp.float32),
        "proj_second": jnp.clip(jnp.exp(math.log(0.01) - 4.6051702 * jax.random.uniform(keys[8], (2 * G * N, D), jnp.float32) ** block_levels(keys[8], (2 * G * N, D), ((0, 4), (1, 8)), -0.2, 0.2)), 0.0001, 0.01),
        "delta_moment": normal_values(keys[9], (H, D), 0.03, 0.2, ((0, 4), (1, 8)), jnp.float32),
        "delta_second": jnp.clip(jnp.exp(math.log(0.01) - 4.6051702 * jax.random.uniform(keys[10], (H, D), jnp.float32) ** block_levels(keys[10], (H, D), ((0, 4), (1, 8)), -0.2, 0.2)), 0.0001, 0.01),
        "doc_lengths": jax.vmap(lambda own: ragged(own, NDOC, SEQ, SEQ // 2, 2))(jax.random.split(keys[11], BATCH)).reshape((BATCH, NDOC)).astype(jnp.int32),
        "valid_counts": draw_valid_counts(jax.random.fold_in(keys[13], 71), 0),
    }


beta_one = 0.9
beta_two = 0.95
adam_eps = 1e-08
adam_step = 100
highest = lax.Precision.HIGHEST

def prepare(inputs, delta, writes, reads, decay_rate, start):
    tokens, heads, width = inputs.shape
    groups = writes.shape[1]
    per_group = heads // groups
    blocks = tokens // Q
    values = inputs.reshape(blocks, Q, groups, per_group, width)
    steps = jnp.transpose(delta.reshape(blocks, Q, groups, per_group), (0, 2, 3, 1))
    write_blocks = writes.reshape(blocks, Q, groups, -1)
    read_blocks = reads.reshape(blocks, Q, groups, -1)
    logs = jnp.cumsum(-decay_rate.reshape(1, groups, per_group, 1) * steps, axis=3)
    marks = jnp.cumsum(start.reshape(blocks, Q), axis=1)
    return (values, steps, write_blocks, read_blocks, logs, marks)

def state_terms(values, steps, write_blocks, logs, marks):
    same_doc = (marks[:, -1:] == marks)[:, None, None, :]
    tail = jnp.where(same_doc, jnp.exp(logs[..., -1:] - logs), 0.0)
    block_states = jnp.einsum('cgjs,csgjp,csgn->cgjpn', tail * steps, values, write_blocks, precision=highest)
    keeps = jnp.where((marks[:, -1] == 0)[:, None, None], jnp.exp(logs[..., -1]), 0.0)
    return (keeps, block_states)

def ssd_forward(inputs, delta, writes, reads, decay_rate, start, state):
    tokens, heads, width = inputs.shape
    values, steps, write_blocks, read_blocks, logs, marks = prepare(inputs, delta, writes, reads, decay_rate, start)
    order = jnp.arange(Q, dtype=jnp.int32)
    inside = (order[:, None] >= order[None, :])[None] & (marks[:, :, None] == marks[:, None, :])
    inside = inside[:, None, None]
    gaps = jnp.where(inside, logs[..., :, None] - logs[..., None, :], 0.0)
    weights = jnp.where(inside, jnp.exp(gaps), 0.0)
    scores = jnp.einsum('ctgn,csgn->cgts', read_blocks, write_blocks, precision=highest)
    mixing = scores[:, :, None] * weights * steps[:, :, :, None, :]
    local_out = jnp.einsum('cgjts,csgjp->ctgjp', mixing, values, precision=highest)
    keeps, block_states = state_terms(values, steps, write_blocks, logs, marks)

    def advance(carry, pair):
        keep, block_state = pair
        return (keep[..., None, None] * carry + block_state, carry)
    final, entering = lax.scan(advance, state, (keeps, block_states))
    head = jnp.where((marks == 0)[:, None, None, :], jnp.exp(logs), 0.0)
    carried_out = jnp.einsum('cgjt,cgjpn,ctgn->ctgjp', head, entering, read_blocks, precision=highest)
    total = local_out + carried_out
    return (total.reshape(tokens, heads, width), final)

def adam_direction(grad, moment, second):
    moment = beta_one * moment + (1.0 - beta_one) * grad
    second = beta_two * second + (1.0 - beta_two) * grad * grad
    corrected = moment / (1.0 - beta_one ** adam_step)
    return corrected / (jnp.sqrt(second / (1.0 - beta_two ** adam_step)) + adam_eps)

def reference(hidden, inputs, upstream, proj_weight, delta_weight, decay_rate, step_bias, proj_moment, proj_second, delta_moment, delta_second, doc_lengths, valid_counts):
    zero_state = jnp.zeros((G, H // G, HEAD_DIM, N), jnp.float32)

    def one_row(carry, row_data):
        rows, row_inputs, row_upstream, lengths, counts = row_data
        projected = jnp.dot(rows, proj_weight.T, preferred_element_type=jnp.float32)
        projected = lax.optimization_barrier(projected.astype(jnp.bfloat16)).astype(jnp.float32)
        mixed = projected.reshape(SEQ, G, 2, N)
        writes = mixed[:, :, 0]
        reads = mixed[:, :, 1]
        raw = jnp.dot(rows, delta_weight.T, preferred_element_type=jnp.float32) + step_bias
        place = jnp.arange(SEQ, dtype=jnp.int32)
        limit = counts[place // TOK_DEV]
        valid = jnp.where(place % TOK_DEV < limit, 1.0, 0.0).astype(jnp.float32)
        starts = (jnp.cumsum(lengths) - lengths).astype(jnp.int32)
        start = jnp.where(jnp.any(place[:, None] == starts[None, :], axis=1), 1.0, 0.0).astype(jnp.float32)
        delta = valid[:, None] * jax.nn.softplus(raw)
        values = row_inputs.astype(jnp.float32).reshape(SEQ, H, HEAD_DIM)
        grads_in = row_upstream.astype(jnp.float32).reshape(SEQ, H, HEAD_DIM) * valid[:, None, None]

        def local(inputs_here, delta_here, writes_here, reads_here, rate_here):
            return ssd_forward(inputs_here, delta_here, writes_here, reads_here, rate_here, start, zero_state)
        unused, pull = jax.vjp(local, values, delta, writes, reads, decay_rate)
        value_grad, delta_grad, write_grad, read_grad, rate_grad = pull((grads_in, zero_state))
        raw_grad = delta_grad * valid[:, None] * jax.nn.sigmoid(raw)
        write_read = jnp.stack([write_grad, read_grad], axis=2).reshape(SEQ, 2 * G * N).astype(jnp.bfloat16)
        raw_round = raw_grad.astype(jnp.bfloat16)
        pieces = write_read.reshape(SEQ, N_TENSOR, -1).astype(jnp.float32)
        weight_pieces = proj_weight.reshape(N_TENSOR, -1, D).astype(jnp.float32)
        raw_pieces = raw_round.reshape(SEQ, N_TENSOR, -1).astype(jnp.float32)
        delta_pieces = delta_weight.reshape(N_TENSOR, -1, D).astype(jnp.float32)
        partial_value = jnp.einsum('tka,kad->ktd', pieces, weight_pieces, precision=highest)
        partial_value = partial_value + jnp.einsum('tka,kad->ktd', raw_pieces, delta_pieces, precision=highest)
        partial_value = lax.optimization_barrier(partial_value.astype(jnp.bfloat16)).astype(jnp.float32)
        hidden_row = lax.optimization_barrier(jnp.sum(partial_value, axis=0)).astype(jnp.bfloat16)
        proj_acc = carry[0] + jnp.dot(write_read.T, rows, preferred_element_type=jnp.float32)
        delta_acc = carry[1] + jnp.dot(raw_round.T, rows, preferred_element_type=jnp.float32)
        head_acc = carry[2] + jnp.stack([rate_grad, lax.optimization_barrier(jnp.sum(raw_grad, axis=0))])
        input_row = value_grad.reshape(SEQ, H * HEAD_DIM).astype(jnp.bfloat16)
        return ((proj_acc, delta_acc, head_acc), (input_row, hidden_row))
    start_carry = (jnp.zeros((2 * G * N, D), jnp.float32), jnp.zeros((H, D), jnp.float32), jnp.zeros((2, H), jnp.float32))
    sums, outputs = lax.scan(one_row, start_carry, (hidden, inputs, upstream, doc_lengths, valid_counts))
    count = jnp.sum(valid_counts).astype(jnp.float32)
    proj_update = adam_direction(sums[0] / count, proj_moment, proj_second)
    delta_update = adam_direction(sums[1] / count, delta_moment, delta_second)
    return (outputs[0], outputs[1], sums[2][0] / count, sums[2][1] / count, proj_update, delta_update)
```

```python
import functools
import jax
import jax.numpy as jnp
from jax import lax
from jax.experimental import pallas as pl
from jax.experimental.pallas import tpu as pltpu
from jax.sharding import PartitionSpec as P

HEAD_DIM = 64
Q = 128
beta_one = 0.9
beta_two = 0.95
adam_eps = 1e-08
adam_step = 100
highest = lax.Precision.HIGHEST
bf16 = jnp.bfloat16
f32 = jnp.float32
NT = (((1,), (1,)), ((), ()))
TN = (((0,), (0,)), ((), ()))


def dot(a, b, dims=(((1,), (0,)), ((), ())), precision=None):
    return lax.dot_general(a, b, dims, precision=precision, preferred_element_type=f32)


def ssd_kernel(parts, ndoc, tok, hp, nstate, info, rate_ref, bias_ref, *refs):
    heads_all = rate_ref.shape[0]
    hw = hp * HEAD_DIM
    per = tok // Q
    nc = parts * per
    pos = 0
    x_in, g_in, m_in, r_in = (refs[i * parts:(i + 1) * parts] for i in range(4))
    pos = 4 * parts
    x_out, m_out, r_out = (refs[pos + i * parts:pos + (i + 1) * parts] for i in range(3))
    pos += 3 * parts
    stats = refs[pos]
    (x_s, g_s, m_s, raw_s, dx_s, dm_s, rg_s, state, adj, enter, delta_s, logs_s, eraw_s, flow_s, spill_s, keep_s, sems) = refs[pos + 1:]
    me = info[0]
    copies = []
    for k in range(parts):
        at = jnp.bitwise_xor(me, k)
        for j, (src, dst) in enumerate(((x_in, x_s), (g_in, g_s), (m_in, m_s), (r_in, raw_s))):
            size = per if dst is raw_s else tok
            copies.append(pltpu.make_async_copy(src[k], dst.at[pl.ds(at * size, size)], sems.at[j * parts + k]))
    for copy in copies:
        copy.start()
    for copy in copies:
        copy.wait()

    lane = lax.broadcasted_iota(jnp.int32, (Q, Q), 1)
    sub = lax.broadcasted_iota(jnp.int32, (Q, Q), 0)
    rlane = lax.broadcasted_iota(jnp.int32, (hp, Q), 1)

    def doc_of(place):
        total = 0
        for k in range(ndoc):
            total = total + jnp.where(place >= info[1 + parts + k], 1, 0)
        return total

    upper = jnp.where(sub <= lane, 1.0, 0.0).astype(f32)
    rate8 = rate_ref[pl.ds(me * hp, hp), :]
    bias8 = bias_ref[pl.ds(me * hp, hp), :]
    rate_all = jnp.concatenate([rate8] * nc, axis=0)
    bias_all = jnp.concatenate([bias8] * nc, axis=0)
    raws, valids = [], []
    for c in range(nc):
        raws.append(raw_s[c, pl.ds(me * hp, hp), :])
        real = info[1 + jnp.bitwise_xor(me, c // per)]
        valids.append(jnp.where(rlane + (c % per) * Q < real, 1.0, 0.0).astype(f32))
    raw_all = jnp.concatenate(raws, axis=0) + bias_all
    valid_all = jnp.concatenate(valids, axis=0)
    small = jnp.exp(-jnp.abs(raw_all))
    soft = jnp.maximum(raw_all, 0.0) + jnp.log1p(small)
    delta_all = valid_all * soft
    logs_all = dot(-rate_all * delta_all, upper, precision=highest)
    delta_s[...] = delta_all.reshape(nc, hp, Q)
    logs_s[...] = logs_all.reshape(nc, hp, Q)

    def rows_of(c):
        base = c * Q
        delta = delta_s[c]
        logs = logs_s[c]
        doc = doc_of(rlane + base)
        last = doc_of(base + Q - 1)
        prev = doc_of(base - 1)
        end = logs[:, Q - 1:Q]
        tail = jnp.where(doc == last, jnp.exp(end - logs), 0.0)
        head = jnp.where(doc == prev, jnp.exp(logs), 0.0)
        keep = jnp.where(last == prev, jnp.exp(end), 0.0)
        return delta, logs, tail, head, keep

    left = lane < HEAD_DIM

    def expand(cols, first):
        out = []
        for a in range(hp // 2):
            one = jnp.broadcast_to(cols[:, first + 2 * a:first + 2 * a + 1], (Q, Q))
            two = jnp.broadcast_to(cols[:, first + 2 * a + 1:first + 2 * a + 2], (Q, Q))
            out.append(jnp.where(left, one, two))
        return jnp.concatenate(out, axis=1)

    def columns(*rows):
        pad = jnp.zeros((Q - len(rows) * hp, Q), f32)
        return jnp.concatenate(rows + (pad,), axis=0).T

    def scaled(ref, keep):
        for h in range(hp):
            band = slice(h * HEAD_DIM, (h + 1) * HEAD_DIM)
            ref[band, :] = ref[band, :] * keep[h:h + 1, :]

    state[...] = jnp.zeros_like(state)
    adj[...] = jnp.zeros_like(adj)

    def forward(c, carry):
        at = pl.ds(pl.multiple_of(c * Q, Q), Q)
        delta, logs, tail, head, keep = rows_of(c)
        enter[c] = state[...].astype(bf16)
        cols = columns(delta * tail)
        weighted = (x_s[at, :].astype(f32) * expand(cols, 0)).astype(bf16)
        scaled(state, keep)
        state[...] += dot(weighted, m_s[at, :nstate], TN)
        return carry

    lax.fori_loop(0, nc, forward, 0)
    eight = (lax.broadcasted_iota(jnp.int32, (hp, hw), 0) == lax.broadcasted_iota(jnp.int32, (hp, hw), 1) // HEAD_DIM)
    eight = jnp.where(eight, 1.0, 0.0).astype(bf16)

    def backward(i, carry):
        c = nc - 1 - i
        at = pl.ds(pl.multiple_of(c * Q, Q), Q)
        delta, logs, tail, head, keep = rows_of(c)
        real = info[1 + jnp.bitwise_xor(me, c // per)]
        x = x_s[at, :]
        wide = lax.broadcasted_iota(jnp.int32, (Q, hw), 0) + (c % per) * Q
        g = jnp.where(wide < real, g_s[at, :].astype(f32), 0.0)
        writes = m_s[at, :nstate]
        reads = m_s[at, nstate:]
        cols = columns(delta, logs, tail, head, delta * tail)
        x32 = x.astype(f32)
        gh = (g * expand(cols, 3 * hp)).astype(bf16)
        xt = (x32 * expand(cols, 4 * hp)).astype(bf16)
        gb = g.astype(bf16)
        before = enter[c]
        after = adj[...].astype(bf16)
        scores = dot(writes, reads, NT)
        scores2 = jnp.concatenate([scores, scores], axis=1)
        same = (doc_of(sub + c * Q) == doc_of(lane + c * Q)) & (lane >= sub)
        shut = jnp.where(same, 0.0, -1e30)
        shut2 = jnp.concatenate([shut, shut], axis=1)
        from_after = dot(writes, after, NT)
        from_before = dot(reads, before, NT)
        acc = jnp.zeros((Q, 2 * Q), f32)
        ecol = jnp.zeros((Q, Q), f32)
        rows, us = [], []
        for a in range(hp // 2):
            band = slice(a * Q, (a + 1) * Q)
            gp = gb[:, band]
            zero = jnp.zeros_like(gp)
            pair = jnp.concatenate([jnp.where(left, gp, zero), jnp.where(left, zero, gp)], axis=0)
            h0, h1 = 2 * a, 2 * a + 1
            lt = jnp.concatenate([logs[h0:h0 + 1, :], logs[h1:h1 + 1, :]], axis=1)
            ls = jnp.concatenate([jnp.broadcast_to(cols[:, hp + h:hp + h + 1], (Q, Q)) for h in (h0, h1)], axis=1)
            ds = jnp.concatenate([jnp.broadcast_to(cols[:, h:h + 1], (Q, Q)) for h in (h0, h1)], axis=1)
            decay = jnp.exp(lt - ls + shut2)
            mixed = decay * scores2
            us.append(dot(mixed.astype(bf16), pair))
            gx = dot(x[:, band], pair, NT)
            acc = acc + decay * gx * ds
            both = mixed * gx
            ecol = jnp.where(lane == h0, jnp.sum(both[:, :Q], axis=1, keepdims=True), ecol)
            ecol = jnp.where(lane == h1, jnp.sum(both[:, Q:], axis=1, keepdims=True), ecol)
            row = jnp.sum(both * ds, axis=0, keepdims=True)
            rows += [row[:, :Q], row[:, Q:]]
        inner = jnp.concatenate(us, axis=1)
        whole = inner + expand(cols, 2 * hp) * from_after
        dx_s[at, :] = (expand(cols, 0) * whole).astype(bf16)
        fold = (acc[:, :Q] + acc[:, Q:]).astype(bf16)
        dm_s[at, :nstate] = (dot(fold, reads) + dot(xt, after)).astype(bf16)
        dm_s[at, nstate:] = (dot(fold, writes, TN) + dot(gh, before)).astype(bf16)
        e_in = ecol.T[:hp, :]
        row_t = jnp.concatenate(rows, axis=0)
        pull_x = dot(eight, (x32 * from_after).astype(bf16), NT)
        pull_g = dot(eight, (g * from_before).astype(bf16), NT)
        eraw_s[c] = e_in + tail * pull_x
        flow_s[c] = row_t - delta * e_in + head * pull_g
        spill_s[c] = delta * tail * pull_x
        both = []
        for h in range(hp):
            band = slice(h * HEAD_DIM, (h + 1) * HEAD_DIM)
            both.append(jnp.sum(adj[band, :] * before[band, :].astype(f32), axis=0, keepdims=True))
        both = jnp.sum(jnp.concatenate(both, axis=0), axis=1, keepdims=True)
        keep_s[c] = jnp.broadcast_to(keep * both, (hp, Q))
        scaled(adj, keep)
        adj[...] += dot(gh, reads, TN)
        return carry

    lax.fori_loop(0, nc, backward, 0)
    flat = lambda ref: ref[...].reshape(nc * hp, Q)
    later = jnp.where(sub >= lane, 1.0, 0.0).astype(f32)
    earlier = jnp.where(sub < lane, 1.0, 0.0).astype(f32)
    log_grad = dot(flat(flow_s), later, precision=highest) + dot(flat(spill_s), earlier, precision=highest) + flat(keep_s)
    sig = jnp.where(raw_all >= 0, 1.0, small) / (1.0 + small)
    raw_grad = (flat(eraw_s) - rate_all * log_grad) * valid_all * sig
    rate_part = -delta_all * log_grad
    rate_sum = jnp.sum(rate_part.reshape(nc, hp, Q), axis=0)
    bias_sum = jnp.sum(raw_grad.reshape(nc, hp, Q), axis=0)
    slane = lax.broadcasted_iota(jnp.int32, (hp, Q), 1)
    stats[...] = jnp.where(slane == 0, jnp.sum(rate_sum, axis=1, keepdims=True), jnp.where(slane == 1, jnp.sum(bias_sum, axis=1, keepdims=True), 0.0))
    mine = lax.broadcasted_iota(jnp.int32, (heads_all, Q), 0) // hp == me
    for c in range(nc):
        block = raw_grad[c * hp:(c + 1) * hp, :]
        spread = jnp.concatenate([block] * (heads_all // hp), axis=0)
        rg_s[c] = jnp.where(mine, spread, 0.0).astype(bf16)
    copies = []
    for k in range(parts):
        at = jnp.bitwise_xor(me, k)
        for j, (src, dst) in enumerate(((dx_s, x_out), (dm_s, m_out), (rg_s, r_out))):
            size = per if src is rg_s else tok
            copies.append(pltpu.make_async_copy(src.at[pl.ds(at * size, size)], dst[k], sems.at[j * parts + k]))
    for copy in copies:
        copy.start()
    for copy in copies:
        copy.wait()


def ssd(info, rate, bias, xs, gs, ms, rs, ndoc):
    parts = len(xs)
    tok, hw = xs[0].shape
    hp = hw // HEAD_DIM
    nstate = ms[0].shape[1] // 2
    heads_all = rate.shape[0]
    per = tok // Q
    nc = parts * per
    total = parts * tok
    anyspec = pl.BlockSpec(memory_space=pl.ANY)
    vm = pl.BlockSpec(memory_space=pltpu.VMEM)
    smem = pl.BlockSpec(memory_space=pltpu.SMEM)
    shape = jax.ShapeDtypeStruct
    outs = ([shape((tok, hw), bf16)] * parts + [shape((tok, 2 * nstate), bf16)] * parts + [shape((per, heads_all, Q), bf16)] * parts + [shape((hp, Q), f32)])
    flops = 2 * total * hw * nstate * 8 + 2 * total * Q * hw * 4
    res = pl.pallas_call(
        functools.partial(ssd_kernel, parts, ndoc, tok, hp, nstate),
        out_shape=outs,
        in_specs=[smem, vm, vm] + [anyspec] * (4 * parts),
        out_specs=[anyspec] * (3 * parts) + [vm],
        scratch_shapes=[
            pltpu.VMEM((total, hw), bf16), pltpu.VMEM((total, hw), bf16), pltpu.VMEM((total, 2 * nstate), bf16), pltpu.VMEM((nc, heads_all, Q), f32),
            pltpu.VMEM((total, hw), bf16), pltpu.VMEM((total, 2 * nstate), bf16), pltpu.VMEM((nc, heads_all, Q), bf16),
            pltpu.VMEM((hw, nstate), f32), pltpu.VMEM((hw, nstate), f32), pltpu.VMEM((nc, hw, nstate), bf16),
            pltpu.VMEM((nc, hp, Q), f32), pltpu.VMEM((nc, hp, Q), f32), pltpu.VMEM((nc, hp, Q), f32), pltpu.VMEM((nc, hp, Q), f32), pltpu.VMEM((nc, hp, Q), f32), pltpu.VMEM((nc, hp, Q), f32),
            pltpu.SemaphoreType.DMA((4 * parts,)),
        ],
        cost_estimate=pl.CostEstimate(flops=flops, bytes_accessed=6 * total * hw * 2, transcendentals=total * Q * hp),
    )(info, rate, bias, *xs, *gs, *ms, *rs)
    return res[:parts], res[parts:2 * parts], res[2 * parts:3 * parts], res[3 * parts]


def adam_direction(grad, moment, second):
    moment = beta_one * moment + (1.0 - beta_one) * grad
    second = beta_two * second + (1.0 - beta_two) * grad * grad
    corrected = moment / (1.0 - beta_one**adam_step)
    return corrected / (jnp.sqrt(second / (1.0 - beta_two**adam_step)) + adam_eps)


def out_kernel(nt, groups, rows, info, *refs):
    m = len(rows)
    flat = sum(rows, ())
    mixed, raws = refs[:nt], refs[nt:2 * nt]
    pieces = refs[2 * nt:2 * nt + len(flat)]
    out = refs[2 * nt + len(flat)]
    mixed_s, raw_s, weight_s, acc, sems = refs[2 * nt + len(flat) + 1:]
    q, t = info[0], info[1]
    first, copies = [], []
    for k in range(nt):
        at = jnp.bitwise_xor(t, k)
        first.append(pltpu.make_async_copy(mixed[k], mixed_s.at[at], sems.at[m]))
        first.append(pltpu.make_async_copy(raws[k], raw_s.at[at], sems.at[m]))
    i = 0
    for r in range(m):
        base, own = 0, []
        for size in rows[r]:
            own.append(pltpu.make_async_copy(pieces[i], weight_s.at[r, pl.ds(base, size)], sems.at[r]))
            base += size
            i += 1
        copies.append(own)
    for copy in first:
        copy.start()
    for own in copies:
        for copy in own:
            copy.start()
    acc[...] = jnp.zeros_like(acc)
    for copy in first:
        copy.wait()
    wide = mixed_s.shape[2]
    per = raw_s.shape[1]
    width = weight_s.shape[2]
    for r in range(m):
        for copy in copies[r]:
            copy.wait()
        src = jnp.bitwise_xor(q, r)
        k, h = src // groups, src % groups
        part = dot(mixed_s[k], weight_s[r, :wide, :])
        tail = [dot(raw_s[k, j], weight_s[r, wide:, :], TN) for j in range(per)]
        acc[h] += part + jnp.concatenate(tail, axis=0)
    for h in range(groups):
        out[:, h * width:(h + 1) * width] = acc[h].astype(out.dtype)


def hidden_gradient(info, mixed, raws, pieces, groups):
    nt, m = len(mixed), len(pieces)
    rows = tuple(tuple(a.shape[0] for a in piece) for piece in pieces)
    width = pieces[0][0].shape[1]
    tok, wide = mixed[0].shape
    height = sum(rows[0])
    flat = [a for piece in pieces for a in piece]
    anyspec = pl.BlockSpec(memory_space=pl.ANY)
    return pl.pallas_call(
        functools.partial(out_kernel, nt, groups, rows),
        out_shape=jax.ShapeDtypeStruct((tok, groups * width), bf16),
        in_specs=[pl.BlockSpec(memory_space=pltpu.SMEM)] + [anyspec] * (2 * nt + len(flat)),
        out_specs=pl.BlockSpec(memory_space=pltpu.VMEM),
        scratch_shapes=[
            pltpu.VMEM((nt, tok, wide), bf16), pltpu.VMEM((nt,) + raws[0].shape, bf16),
            pltpu.VMEM((m, height, width), bf16), pltpu.VMEM((groups, tok, width), f32),
            pltpu.SemaphoreType.DMA((m + 1,)),
        ],
        cost_estimate=pl.CostEstimate(flops=2 * m * tok * height * width, bytes_accessed=2 * m * height * width, transcendentals=0),
    )(info, *mixed, *raws, *flat)


def shards(hidden, inputs, upstream, proj_weight, delta_weight, decay_rate, step_bias, proj_moment, proj_second,
           delta_moment, delta_second, doc_lengths, valid_counts):
    nd, nx, nt = (lax.axis_size(a) for a in ("dp", "context", "tensor"))
    m = nd * nx
    d, c, t = (lax.axis_index(a) for a in ("dp", "context", "tensor"))
    p = d * nx + c
    tok, model = hidden.shape[1:]
    heads = decay_rate.shape[0]
    wide = proj_weight.shape[0]
    nstate = wide // 2
    width = model // m
    hw = inputs.shape[2] // nx
    per = tok // Q
    groups = m // nt
    ndoc = doc_lengths.shape[1]
    plane = ("dp", "context")

    def over_plane(x, r):
        return lax.ppermute(x, plane, [(i, i ^ r) for i in range(m)])

    def over_context(x, r):
        return lax.ppermute(x, "context", [(i, i ^ r) for i in range(nx)])

    def over_dp(x, r):
        return lax.ppermute(x, "dp", [(i, i ^ r) for i in range(nd)])

    def over_tensor(x, r):
        return lax.ppermute(x, "tensor", [(i, i ^ r) for i in range(nt)])

    def after(value, *first):
        return lax.optimization_barrier((value, first))[0]

    rows = hidden[0]
    columns = []
    for r in range(m):
        piece = lax.dynamic_slice_in_dim(rows, (p ^ r) * width, width, axis=1)
        columns.append(over_plane(piece, r) if r else piece)
    counts = [valid_counts[0] if r == 0 else over_context(valid_counts[0], r) for r in range(nx)]
    total_count = sum(counts)
    total_count = total_count + sum(over_dp(total_count, r) for r in range(1, nd))
    count = total_count[0].astype(f32)

    parts, raw_parts = [], []
    for r in range(m):
        parts.append(lax.dot_general(columns[r], proj_weight, NT, preferred_element_type=f32).astype(bf16))
        raw = lax.dot_general(delta_weight, columns[r], NT, preferred_element_type=f32)
        raw_parts.append(jnp.transpose(raw.reshape(heads, per, Q), (1, 0, 2)))

    gate = columns[m - 1]
    xs, gs = [], []
    for r in range(nx):
        for source, held in ((inputs, xs), (upstream, gs)):
            piece = lax.dynamic_slice_in_dim(source[0], (c ^ r) * hw, hw, axis=1)
            if r:
                piece = over_context(after(piece, gate), r)
            held.append(piece)

    own = jnp.concatenate([proj_weight, delta_weight], axis=0)
    moves = [(a * nt + k, (k * groups + a % groups) * nt + a // groups) for a in range(m) for k in range(nt)]
    own = lax.ppermute(after(own, gate), plane + ("tensor",), moves)

    def reduced(pieces):
        kept = pieces[:nx]
        for r in range(1, nd):
            came = [over_dp(pieces[r * nx + k], r) for k in range(nx)]
            kept = [a.astype(f32) + b.astype(f32) for a, b in zip(kept, came)]
        kept = [a.astype(pieces[0].dtype) for a in kept]
        total = kept[0].astype(f32)
        for k in range(1, nx):
            total = total + over_context(kept[k], k).astype(f32)
        return total

    projected = reduced(parts).astype(bf16)
    raw = reduced(raw_parts)
    mixed = [projected] + [over_context(projected, k) for k in range(1, nx)]
    raws = [raw] + [over_context(raw, k) for k in range(1, nx)]

    starts = jnp.cumsum(doc_lengths[0]) - doc_lengths[0]
    info = jnp.concatenate([jnp.reshape(c, (1,))] + [jnp.reshape(v, (1,)) for v in counts] + [starts]).astype(jnp.int32)
    value_parts, mixed_parts, raw_grads, stats = ssd(info, decay_rate[:, None], step_bias[:, None], xs, gs, mixed, raws, ndoc)

    own = after(own, mixed[nx - 1], xs[nx - 1], gs[nx - 1])
    height = own.shape[0]
    if nx == 4:
        one, two = over_context(own, 1), over_context(own, 2)
        one_late, two_late = after((one, two), mixed_parts[0])
        cut = height // 2
        three = (over_context(one_late[:cut], 2), over_context(two_late[cut:], 1))
        pieces = [(own,), (one,), (two,), three]
    else:
        pieces = [(own,)] + [(over_context(own, k),) for k in range(1, nx)]
    for r in range(1, nd):
        pieces += [tuple(over_dp(a, r) for a in piece) for piece in pieces[:nx]]

    wr = mixed_parts[0].astype(f32)
    rr = raw_grads[0].astype(f32)
    for k in range(1, nx):
        wr = wr + over_context(mixed_parts[k], k).astype(f32)
        rr = rr + over_context(raw_grads[k], k).astype(f32)
    wr, rr = wr.astype(bf16), rr.astype(bf16)
    wr_groups = [wr] + [over_tensor(wr, k) for k in range(1, nt)]
    rr_groups = [rr] + [over_tensor(rr, k) for k in range(1, nt)]
    hidden_grad = hidden_gradient(jnp.stack([p, t]).astype(jnp.int32), wr_groups, rr_groups, pieces, groups)

    def gathered(x):
        have = [x] + [over_context(x, k) for k in range(1, nx)]
        for r in range(1, nd):
            have += [over_dp(a, r) for a in have[:nx]]
        return have

    wr_all = jnp.concatenate(gathered(wr), axis=0)
    rr_all = jnp.concatenate(gathered(rr), axis=0)
    rr_all = jnp.transpose(rr_all, (1, 0, 2)).reshape(heads, m * tok)
    whole = jnp.concatenate(columns, axis=0)
    proj_next = lax.dot_general(wr_all, whole, TN, preferred_element_type=f32)
    delta_next = lax.dot_general(rr_all, whole, (((1,), (0,)), ((), ())), preferred_element_type=f32)
    proj_update = adam_direction(proj_next / count, proj_moment, proj_second)
    delta_update = adam_direction(delta_next / count, delta_moment, delta_second)

    back = [value_parts[0]] + [over_context(value_parts[k], k) for k in range(1, nx)]
    input_grad = jnp.zeros((tok, nx * hw), bf16)
    for k in range(nx):
        input_grad = lax.dynamic_update_slice_in_dim(input_grad, back[k], (c ^ k) * hw, axis=1)

    sums = stats
    for r in range(1, nd):
        sums = sums + over_dp(stats, r)
    hp = heads // nx
    spread = jnp.zeros((nx, hp, 2), f32)
    for k in range(nx):
        piece = (sums if k == 0 else over_context(sums, k))[:, :2]
        spread = lax.dynamic_update_slice_in_dim(spread, piece[None], c ^ k, axis=0)
    head_sum = spread.reshape(heads, 2) / count
    return input_grad[None], hidden_grad[None], head_sum[:, 0], head_sum[:, 1], proj_update, delta_update


def solution(mesh):
    whole = ("dp", "context")
    return jax.shard_map(
        shards,
        mesh=mesh,
        in_specs=(
            P("dp", "context", None), P("dp", "context", "tensor"), P("dp", "context", "tensor"),
            P("tensor", whole), P("tensor", whole), P("tensor"), P("tensor"),
            P("tensor", whole), P("tensor", whole), P("tensor", whole), P("tensor", whole),
            P("dp", None), P("dp", "context"),
        ),
        out_specs=(
            P("dp", "context", "tensor"), P("dp", "context", "tensor"), P("tensor"), P("tensor"),
            P("tensor", whole), P("tensor", whole),
        ),
        check_vma=False,
    )
```

```python
import functools
import jax
import jax.numpy as jnp
from jax import lax
from jax.experimental import pallas as pl
from jax.experimental.pallas import tpu as pltpu
from jax.sharding import PartitionSpec as P

HEAD_DIM = 64
Q = 128
beta_one = 0.9
beta_two = 0.95
adam_eps = 1e-08
adam_step = 100
closed = -1e30
highest = lax.Precision.HIGHEST
bf16 = jnp.bfloat16
f32 = jnp.float32
NT = (((1,), (1,)), ((), ()))
TN = (((0,), (0,)), ((), ()))


def dot(a, b, dims=(((1,), (0,)), ((), ())), precision=None):
    return lax.dot_general(a, b, dims, precision=precision, preferred_element_type=f32)


def ssd_kernel(parts, ndoc, tok, hp, nstate, info, rate_ref, bias_ref, *refs):
    heads_all = rate_ref.shape[0]
    hw = hp * HEAD_DIM
    per = tok // Q
    nc = parts * per
    x_in, m_in = (refs[i * parts:(i + 1) * parts] for i in range(2))
    pos = 2 * parts
    x_out, m_out = (refs[pos + i * parts:pos + (i + 1) * parts] for i in range(2))
    pos += 2 * parts
    (x_s, g_s, m_s, raw_s, dx_s, dm_s, rg_s, state, adj, enter, delta_s, logs_s, eraw_s, flow_s, spill_s, keep_s, sems) = refs[pos:]
    me = info[0]
    copies = []
    for k in range(parts):
        at = jnp.bitwise_xor(me, k)
        rows = pl.ds(at * tok, tok)
        copies.append(pltpu.make_async_copy(x_in[k].at[pl.ds(0, tok)], x_s.at[rows], sems.at[k]))
        copies.append(pltpu.make_async_copy(x_in[k].at[pl.ds(tok, tok)], g_s.at[rows], sems.at[parts + k]))
        copies.append(pltpu.make_async_copy(m_in[k].at[pl.ds(0, tok)], m_s.at[rows], sems.at[2 * parts + k]))
        copies.append(pltpu.make_async_copy(m_in[k].at[pl.ds(tok, heads_all)], raw_s.at[at], sems.at[3 * parts + k]))
    for copy in copies:
        copy.start()
    for copy in copies:
        copy.wait()

    lane = lax.broadcasted_iota(jnp.int32, (Q, Q), 1)
    sub = lax.broadcasted_iota(jnp.int32, (Q, Q), 0)
    rlane = lax.broadcasted_iota(jnp.int32, (hp, Q), 1)

    def doc_of(place):
        total = 0
        for k in range(ndoc):
            total = total + jnp.where(place >= info[1 + k], 1, 0)
        return total

    upper = jnp.where(sub <= lane, 1.0, 0.0).astype(f32)
    rate8 = rate_ref[pl.ds(me * hp, hp), :]
    bias8 = bias_ref[pl.ds(me * hp, hp), :]
    rate_all = jnp.concatenate([rate8] * nc, axis=0)
    bias_all = jnp.concatenate([bias8] * nc, axis=0)
    raws = []
    for c in range(nc):
        first = (c % per) * Q
        block = raw_s[c // per, :, first:first + Q].astype(f32) + raw_s[c // per, :, tok + first:tok + first + Q].astype(f32)
        mine = jnp.zeros((hp, Q), f32)
        for j in range(parts):
            mine = jnp.where(me == j, block[j * hp:(j + 1) * hp, :], mine)
        raws.append(mine)
    raw_all = jnp.concatenate(raws, axis=0) + bias_all
    small = jnp.exp(-jnp.abs(raw_all))
    soft = jnp.maximum(raw_all, 0.0) + jnp.log1p(small)
    delta_all = soft
    logs_all = dot(-rate_all * delta_all, upper, precision=highest)
    delta_s[...] = delta_all.reshape(nc, hp, Q)
    logs_s[...] = logs_all.reshape(nc, hp, Q)

    def rows_of(c):
        base = c * Q
        delta = delta_s[c]
        logs = logs_s[c]
        doc = doc_of(rlane + base)
        last = doc_of(base + Q - 1)
        prev = doc_of(base - 1)
        end = logs[:, Q - 1:Q]
        tail = jnp.where(doc == last, jnp.exp(end - logs), 0.0)
        head = jnp.where(doc == prev, jnp.exp(logs), 0.0)
        keep = jnp.where(last == prev, jnp.exp(end), 0.0)
        return delta, logs, tail, head, keep

    left = lane < HEAD_DIM

    def expand(cols, first):
        out = []
        for a in range(hp // 2):
            one = jnp.broadcast_to(cols[:, first + 2 * a:first + 2 * a + 1], (Q, Q))
            two = jnp.broadcast_to(cols[:, first + 2 * a + 1:first + 2 * a + 2], (Q, Q))
            out.append(jnp.where(left, one, two))
        return jnp.concatenate(out, axis=1)

    def columns(*rows):
        pad = jnp.zeros((Q - len(rows) * hp, Q), f32)
        return jnp.concatenate(rows + (pad,), axis=0).T

    def scaled(ref, keep):
        for h in range(hp):
            band = slice(h * HEAD_DIM, (h + 1) * HEAD_DIM)
            ref[band, :] = ref[band, :] * keep[h:h + 1, :]

    state[...] = jnp.zeros_like(state)
    adj[...] = jnp.zeros_like(adj)

    def forward(c, carry):
        at = pl.ds(pl.multiple_of(c * Q, Q), Q)
        delta, logs, tail, head, keep = rows_of(c)
        enter[c] = state[...].astype(bf16)
        cols = columns(delta * tail)
        weighted = (x_s[at, :].astype(f32) * expand(cols, 0)).astype(bf16)
        scaled(state, keep)
        state[...] += dot(weighted, m_s[at, :nstate], TN)
        return carry

    lax.fori_loop(0, nc, forward, 0)
    eight = (lax.broadcasted_iota(jnp.int32, (hp, hw), 0) == lax.broadcasted_iota(jnp.int32, (hp, hw), 1) // HEAD_DIM)
    eight = jnp.where(eight, 1.0, 0.0).astype(bf16)

    def backward(i, carry):
        c = nc - 1 - i
        at = pl.ds(pl.multiple_of(c * Q, Q), Q)
        delta, logs, tail, head, keep = rows_of(c)
        x = x_s[at, :]
        gb = g_s[at, :]
        g = gb.astype(f32)
        writes = m_s[at, :nstate]
        reads = m_s[at, nstate:]
        cols = columns(delta, logs, tail, head, delta * tail)
        x32 = x.astype(f32)
        gh = (g * expand(cols, 3 * hp)).astype(bf16)
        xt = (x32 * expand(cols, 4 * hp)).astype(bf16)
        before = enter[c]
        after = adj[...].astype(bf16)
        scores = dot(writes, reads, NT)
        scores2 = jnp.concatenate([scores, scores], axis=1)
        same = (doc_of(sub + c * Q) == doc_of(lane + c * Q)) & (lane >= sub)
        shut = jnp.where(same, 0.0, -1e30)
        shut2 = jnp.concatenate([shut, shut], axis=1)
        from_after = dot(writes, after, NT)
        from_before = dot(reads, before, NT)
        acc = jnp.zeros((Q, 2 * Q), f32)
        ecol = jnp.zeros((Q, Q), f32)
        rows, us = [], []
        for a in range(hp // 2):
            band = slice(a * Q, (a + 1) * Q)
            gp = gb[:, band]
            zero = jnp.zeros_like(gp)
            pair = jnp.concatenate([jnp.where(left, gp, zero), jnp.where(left, zero, gp)], axis=0)
            h0, h1 = 2 * a, 2 * a + 1
            lt = jnp.concatenate([logs[h0:h0 + 1, :], logs[h1:h1 + 1, :]], axis=1)
            ls = jnp.concatenate([jnp.broadcast_to(cols[:, hp + h:hp + h + 1], (Q, Q)) for h in (h0, h1)], axis=1)
            ds = jnp.concatenate([jnp.broadcast_to(cols[:, h:h + 1], (Q, Q)) for h in (h0, h1)], axis=1)
            decay = jnp.exp(lt - ls + shut2)
            mixed = decay * scores2
            us.append(dot(mixed.astype(bf16), pair))
            gx = dot(x[:, band], pair, NT)
            acc = acc + decay * gx * ds
            both = mixed * gx
            ecol = jnp.where(lane == h0, jnp.sum(both[:, :Q], axis=1, keepdims=True), ecol)
            ecol = jnp.where(lane == h1, jnp.sum(both[:, Q:], axis=1, keepdims=True), ecol)
            row = jnp.sum(both * ds, axis=0, keepdims=True)
            rows += [row[:, :Q], row[:, Q:]]
        inner = jnp.concatenate(us, axis=1)
        whole = inner + expand(cols, 2 * hp) * from_after
        dx_s[at, :] = (expand(cols, 0) * whole).astype(bf16)
        fold = (acc[:, :Q] + acc[:, Q:]).astype(bf16)
        dm_s[at, :nstate] = (dot(fold, reads) + dot(xt, after)).astype(bf16)
        dm_s[at, nstate:] = (dot(fold, writes, TN) + dot(gh, before)).astype(bf16)
        e_in = ecol.T[:hp, :]
        row_t = jnp.concatenate(rows, axis=0)
        pull_x = dot(eight, (x32 * from_after).astype(bf16), NT)
        pull_g = dot(eight, (g * from_before).astype(bf16), NT)
        eraw_s[c] = e_in + tail * pull_x
        flow_s[c] = row_t - delta * e_in + head * pull_g
        spill_s[c] = delta * tail * pull_x
        both = []
        for h in range(hp):
            band = slice(h * HEAD_DIM, (h + 1) * HEAD_DIM)
            both.append(jnp.sum(adj[band, :] * before[band, :].astype(f32), axis=0, keepdims=True))
        both = jnp.sum(jnp.concatenate(both, axis=0), axis=1, keepdims=True)
        keep_s[c] = jnp.broadcast_to(keep * both, (hp, Q))
        scaled(adj, keep)
        adj[...] += dot(gh, reads, TN)
        return carry

    lax.fori_loop(0, nc, backward, 0)
    flat = lambda ref: ref[...].reshape(nc * hp, Q)
    later = jnp.where(sub >= lane, 1.0, 0.0).astype(f32)
    earlier = jnp.where(sub < lane, 1.0, 0.0).astype(f32)
    log_grad = dot(flat(flow_s), later, precision=highest) + dot(flat(spill_s), earlier, precision=highest) + flat(keep_s)
    sig = jnp.where(raw_all >= 0, 1.0, small) / (1.0 + small)
    raw_grad = (flat(eraw_s) - rate_all * log_grad) * sig
    rate_part = -delta_all * log_grad
    rate_sum = jnp.sum(rate_part.reshape(nc, hp, Q), axis=0)
    bias_sum = jnp.sum(raw_grad.reshape(nc, hp, Q), axis=0)
    rate_sum = jnp.sum(rate_sum, axis=1, keepdims=True)
    bias_sum = jnp.sum(bias_sum, axis=1, keepdims=True)
    mine = lax.broadcasted_iota(jnp.int32, (heads_all, Q), 0) // hp == me
    slane = lax.broadcasted_iota(jnp.int32, (hp, Q), 1)
    values = []
    for value in (rate_sum, bias_sum):
        high = value.astype(bf16).astype(f32)
        values += [high, value - high]
    sums = jnp.zeros((hp, Q), f32)
    for k, value in enumerate(values):
        sums = jnp.where(slane == k, value, sums)

    def spread(block):
        return jnp.where(mine, jnp.concatenate([block] * (heads_all // hp), axis=0), 0.0).astype(bf16)

    rg_s[...] = jnp.zeros_like(rg_s)
    for c in range(nc):
        first = (c % per) * Q
        rg_s[c // per, :, first:first + Q] = spread(raw_grad[c * hp:(c + 1) * hp, :])
    for b in range(parts):
        rg_s[b, :, tok:tok + Q] = spread(sums)
    copies = []
    for k in range(parts):
        at = jnp.bitwise_xor(me, k)
        rows = pl.ds(at * tok, tok)
        copies.append(pltpu.make_async_copy(dx_s.at[rows], x_out[k], sems.at[k]))
        copies.append(pltpu.make_async_copy(dm_s.at[rows], m_out[k].at[pl.ds(0, tok)], sems.at[parts + k]))
        copies.append(pltpu.make_async_copy(rg_s.at[at], m_out[k].at[pl.ds(tok, heads_all)], sems.at[2 * parts + k]))
    for copy in copies:
        copy.start()
    for copy in copies:
        copy.wait()


def ssd(info, rate, bias, xs, ms, ndoc):
    parts = len(xs)
    tok, hw = xs[0].shape[0] // 2, xs[0].shape[1]
    hp = hw // HEAD_DIM
    nstate = ms[0].shape[1] // 2
    heads_all = rate.shape[0]
    per = tok // Q
    nc = parts * per
    total = parts * tok
    anyspec = pl.BlockSpec(memory_space=pl.ANY)
    vm = pl.BlockSpec(memory_space=pltpu.VMEM)
    smem = pl.BlockSpec(memory_space=pltpu.SMEM)
    shape = jax.ShapeDtypeStruct
    outs = [shape((tok, hw), bf16)] * parts + [shape((tok + heads_all, 2 * nstate), bf16)] * parts
    flops = 2 * total * hw * nstate * 8 + 2 * total * Q * hw * 4
    res = pl.pallas_call(
        functools.partial(ssd_kernel, parts, ndoc, tok, hp, nstate),
        out_shape=outs,
        in_specs=[smem, vm, vm] + [anyspec] * (2 * parts),
        out_specs=[anyspec] * (2 * parts),
        scratch_shapes=[
            pltpu.VMEM((total, hw), bf16), pltpu.VMEM((total, hw), bf16), pltpu.VMEM((total, 2 * nstate), bf16), pltpu.VMEM((parts, heads_all, 2 * nstate), bf16),
            pltpu.VMEM((total, hw), bf16), pltpu.VMEM((total, 2 * nstate), bf16), pltpu.VMEM((parts, heads_all, 2 * nstate), bf16),
            pltpu.VMEM((hw, nstate), f32), pltpu.VMEM((hw, nstate), f32), pltpu.VMEM((nc, hw, nstate), bf16),
            pltpu.VMEM((nc, hp, Q), f32), pltpu.VMEM((nc, hp, Q), f32), pltpu.VMEM((nc, hp, Q), f32), pltpu.VMEM((nc, hp, Q), f32), pltpu.VMEM((nc, hp, Q), f32), pltpu.VMEM((nc, hp, Q), f32),
            pltpu.SemaphoreType.DMA((4 * parts,)),
        ],
        cost_estimate=pl.CostEstimate(flops=flops, bytes_accessed=6 * total * hw * 2, transcendentals=total * Q * hp),
    )(info, rate, bias, *xs, *ms)
    return res[:parts], res[parts:]


anyspec = pl.BlockSpec(memory_space=pl.ANY)
vmspec = pl.BlockSpec(memory_space=pltpu.VMEM)
smspec = pl.BlockSpec(memory_space=pltpu.SMEM)


def halves(value):
    high = value.astype(bf16)
    return jnp.concatenate([high, (value - high.astype(f32)).astype(bf16)], axis=1)


def joined(block):
    wide = block.shape[1] // 2
    return block[:, :wide].astype(f32) + block[:, wide:].astype(f32)


def project_kernel(count, weight_ref, step_ref, *refs):
    pieces, out, held, sems = refs[:count], refs[count], refs[count + 1], refs[count + 2]
    tok = held.shape[1]
    copies = [pltpu.make_async_copy(pieces[k], held.at[k], sems.at[k]) for k in range(count)]
    for copy in copies:
        copy.start()
    weight, step = weight_ref[...], step_ref[...]
    for k in range(count):
        copies[k].wait()
        rows = held[k]
        out[k, :tok, :] = dot(rows, weight, NT).astype(bf16)
        out[k, tok:, :] = halves(dot(step, rows, NT))


def project(pieces, weight, step):
    count = len(pieces)
    tok, width = pieces[0].shape
    wide, heads = weight.shape[0], step.shape[0]
    assert wide == 2 * tok
    return pl.pallas_call(
        functools.partial(project_kernel, count),
        out_shape=jax.ShapeDtypeStruct((count, tok + heads, wide), bf16),
        in_specs=[vmspec, vmspec] + [anyspec] * count,
        out_specs=vmspec,
        scratch_shapes=[pltpu.VMEM((count, tok, width), bf16), pltpu.SemaphoreType.DMA((count,))],
        cost_estimate=pl.CostEstimate(flops=2 * count * tok * width * wide, bytes_accessed=2 * count * tok * width, transcendentals=0),
    )(weight, step, *pieces)


def pair_kernel(count, others, *refs):
    own, came, outs = refs[0], refs[1:1 + others], refs[1 + others:]
    heads = outs[0].shape[0] - outs[0].shape[1] // 2
    tok = outs[0].shape[1] // 2
    for k in range(count):
        total, raw = own[k, :tok, :].astype(f32), joined(own[k, tok:, :])
        for other in came:
            total = total + other[k, :tok, :].astype(f32)
            raw = raw + joined(other[k, tok:, :])
        outs[k][:tok, :] = total.astype(bf16)
        outs[k][tok:, :] = halves(raw)


def pair_sum(own, came):
    count = own.shape[0]
    return pl.pallas_call(
        functools.partial(pair_kernel, count, len(came)),
        out_shape=[jax.ShapeDtypeStruct(own.shape[1:], bf16)] * count,
        in_specs=[vmspec] * (1 + len(came)),
        out_specs=[vmspec] * count,
    )(own, *came)


def total_kernel(count, real, *refs):
    pieces, out = refs[:count], refs[count]
    tok = out.shape[1] // 2
    heads = out.shape[0] - tok
    total, raw = pieces[0][:tok, :].astype(f32), joined(pieces[0][tok:, :])
    for piece in pieces[1:]:
        total = total + piece[:tok, :].astype(f32)
        raw = raw + joined(piece[tok:, :])
    place = lax.broadcasted_iota(jnp.int32, (heads, tok), 1)
    raw = jnp.where(place < real[0], raw, closed)
    out[:tok, :] = total.astype(bf16)
    out[tok:, :] = halves(raw)


def token_sum(pieces, real):
    return pl.pallas_call(
        functools.partial(total_kernel, len(pieces)),
        out_shape=jax.ShapeDtypeStruct(pieces[0].shape, bf16),
        in_specs=[smspec] + [vmspec] * len(pieces),
        out_specs=vmspec,
    )(real, *pieces)


def grads_kernel(count, real, *refs):
    pieces, out = refs[:count], refs[count]
    tok = out.shape[1] // 2
    total = pieces[0][...].astype(f32)
    for piece in pieces[1:]:
        total = total + piece[...].astype(f32)
    out[...] = total.astype(bf16)
    lane = lax.broadcasted_iota(jnp.int32, (out.shape[0] - tok, Q), 1)
    whole, rest = (real[0] // 16).astype(f32), (real[0] % 16).astype(f32)
    extra = jnp.where(lane == 4, whole, jnp.where(lane == 5, rest, 0.0))
    out[tok:, tok:tok + Q] = (total[tok:, tok:tok + Q] + extra).astype(bf16)


def gradient_sum(pieces, real):
    return pl.pallas_call(
        functools.partial(grads_kernel, len(pieces)),
        out_shape=jax.ShapeDtypeStruct(pieces[0].shape, bf16),
        in_specs=[smspec] + [vmspec] * len(pieces),
        out_specs=vmspec,
    )(real, *pieces)


def adam_direction(grad, moment, second):
    moment = beta_one * moment + (1.0 - beta_one) * grad
    second = beta_two * second + (1.0 - beta_two) * grad * grad
    corrected = moment / (1.0 - beta_one**adam_step)
    return corrected / (jnp.sqrt(second / (1.0 - beta_two**adam_step)) + adam_eps)


def update_kernel(m, nd, *refs):
    pieces, columns = refs[:m], refs[m:2 * m]
    moments, out, step_out, sums = refs[2 * m:2 * m + 4], refs[2 * m + 4], refs[2 * m + 5], refs[2 * m + 6]
    held, cols, acc, step_acc, sems = refs[2 * m + 7:]
    tok = columns[0].shape[0]
    copies = []
    for r in range(m):
        copies.append((pltpu.make_async_copy(pieces[r], held.at[r], sems.at[r]), pltpu.make_async_copy(columns[r], cols.at[r], sems.at[m + r])))
    for pair in copies:
        for copy in pair:
            copy.start()
    for r in range(m):
        for copy in copies[r]:
            copy.wait()
        part = dot(held[r, :tok, :], cols[r], TN)
        step = dot(held[r, tok:, :tok], cols[r])
        if r:
            acc[...] += part
            step_acc[...] += step
        else:
            acc[...] = part
            step_acc[...] = step
    stat = [held[r, tok:, tok:tok + Q].astype(f32) for r in range(m)]
    both = sum(stat)
    count = both[0:1, 4:5] * 16.0 + both[0:1, 5:6]
    mine = sum(stat[r] for r in range(0, m, m // nd))
    lane = lax.broadcasted_iota(jnp.int32, mine.shape, 1)
    rate = (mine[:, 0:1] + mine[:, 1:2]) / count
    bias = (mine[:, 2:3] + mine[:, 3:4]) / count
    sums[...] = jnp.where(lane == 0, rate, bias)
    high = 64
    for k in range(acc.shape[0] // high):
        band = slice(k * high, (k + 1) * high)
        out[band, :] = adam_direction(acc[band, :] / count, moments[0][band, :], moments[1][band, :])
    step_out[...] = adam_direction(step_acc[...] / count, moments[2][...], moments[3][...])


def update(pieces, columns, moments, nd):
    m = len(pieces)
    tok, width = columns[0].shape
    height, wide = pieces[0].shape
    heads = height - tok
    shape = jax.ShapeDtypeStruct
    return pl.pallas_call(
        functools.partial(update_kernel, m, nd),
        out_shape=[shape((wide, width), f32), shape((heads, width), f32), shape((heads, Q), f32)],
        in_specs=[anyspec] * (2 * m) + [vmspec] * 4,
        out_specs=[vmspec] * 3,
        scratch_shapes=[
            pltpu.VMEM((m, height, wide), bf16), pltpu.VMEM((m, tok, width), bf16),
            pltpu.VMEM((wide, width), f32), pltpu.VMEM((heads, width), f32), pltpu.SemaphoreType.DMA((2 * m,)),
        ],
        cost_estimate=pl.CostEstimate(flops=2 * m * tok * width * wide, bytes_accessed=12 * wide * width + 2 * m * tok * width, transcendentals=0),
    )(*pieces, *columns, *moments)


def out_kernel(nt, nx, groups, rows, info, *refs):
    m = len(rows)
    flat = sum(rows, ())
    mixed, values = refs[:nt], refs[nt:nt + nx]
    pieces = refs[nt + nx:nt + nx + len(flat)]
    out, value_out = refs[nt + nx + len(flat):nt + nx + len(flat) + 2]
    held, weight_s, acc, sems = refs[nt + nx + len(flat) + 2:]
    q, t, c = info[0], info[1], info[2]
    first, copies = [], []
    for k in range(nt):
        first.append(pltpu.make_async_copy(mixed[k], held.at[jnp.bitwise_xor(t, k)], sems.at[m + k]))
    hw = values[0].shape[1]
    for k in range(nx):
        place = pl.ds(pl.multiple_of(jnp.bitwise_xor(c, k) * hw, hw), hw)
        first.append(pltpu.make_async_copy(values[k], value_out.at[:, place], sems.at[m + nt + k]))
    i = 0
    for r in range(m):
        base, own = 0, []
        for size in rows[r]:
            own.append(pltpu.make_async_copy(pieces[i], weight_s.at[r, pl.ds(base, size)], sems.at[r]))
            base += size
            i += 1
        copies.append(own)
    for copy in first[:nt]:
        copy.start()
    for own in copies:
        for copy in own:
            copy.start()
    for copy in first[nt:]:
        copy.start()
    acc[...] = jnp.zeros_like(acc)
    for copy in first[:nt]:
        copy.wait()
    wide = held.shape[2]
    tok = out.shape[0]
    width = weight_s.shape[2]
    for r in range(m):
        for copy in copies[r]:
            copy.wait()
        src = jnp.bitwise_xor(q, r)
        k, h = src // groups, src % groups
        acc[h] += dot(held[k, :tok, :], weight_s[r, :wide, :]) + dot(held[k, tok:, :tok], weight_s[r, wide:, :], TN)
    for h in range(groups):
        out[:, h * width:(h + 1) * width] = acc[h].astype(out.dtype)
    for copy in first[nt:]:
        copy.wait()


def hidden_gradient(info, mixed, values, pieces, groups):
    nt, nx, m = len(mixed), len(values), len(pieces)
    rows = tuple(tuple(a.shape[0] for a in piece) for piece in pieces)
    width = pieces[0][0].shape[1]
    tok, hw = values[0].shape
    height = sum(rows[0])
    flat = [a for piece in pieces for a in piece]
    return pl.pallas_call(
        functools.partial(out_kernel, nt, nx, groups, rows),
        out_shape=[jax.ShapeDtypeStruct((tok, groups * width), bf16), jax.ShapeDtypeStruct((tok, nx * hw), bf16)],
        in_specs=[smspec] + [anyspec] * (nt + nx + len(flat)),
        out_specs=[vmspec, vmspec],
        scratch_shapes=[
            pltpu.VMEM((nt,) + mixed[0].shape, bf16),
            pltpu.VMEM((m, height, width), bf16), pltpu.VMEM((groups, tok, width), f32),
            pltpu.SemaphoreType.DMA((m + nt + nx,)),
        ],
        cost_estimate=pl.CostEstimate(flops=2 * m * tok * height * width, bytes_accessed=2 * m * height * width, transcendentals=0),
    )(info, *mixed, *values, *flat)


def shards(hidden, inputs, upstream, proj_weight, delta_weight, decay_rate, step_bias, proj_moment, proj_second,
           delta_moment, delta_second, doc_lengths, valid_counts):
    nd, nx, nt = (lax.axis_size(a) for a in ("dp", "context", "tensor"))
    m = nd * nx
    d, c, t = (lax.axis_index(a) for a in ("dp", "context", "tensor"))
    p = d * nx + c
    tok, model = hidden.shape[1:]
    width = model // m
    hw = inputs.shape[2] // nx
    groups = m // nt
    ndoc = doc_lengths.shape[1]
    plane = ("dp", "context")
    real = valid_counts[0]

    def over_plane(x, r):
        return lax.ppermute(x, plane, [(i, i ^ r) for i in range(m)])

    def over_context(x, r):
        return lax.ppermute(x, "context", [(i, i ^ r) for i in range(nx)])

    def over_dp(x, r):
        return lax.ppermute(x, "dp", [(i, i ^ r) for i in range(nd)])

    def over_tensor(x, r):
        return lax.ppermute(x, "tensor", [(i, i ^ r) for i in range(nt)])

    def after(value, *first):
        return lax.optimization_barrier((value, first))[0]

    rows = hidden[0]
    columns = [None] * m
    for r in list(range(nx, m)) + list(range(nx)):
        piece = lax.dynamic_slice_in_dim(rows, (p ^ r) * width, width, axis=1)
        columns[r] = over_plane(piece, r) if r else piece

    came = []
    for r in range(1, nd):
        came.append(over_dp(project(columns[r * nx:(r + 1) * nx], proj_weight, delta_weight), r))
    pieces = pair_sum(project(columns[:nx], proj_weight, delta_weight), came)
    gate = columns[nx - 1]

    ahead = jnp.where(jnp.arange(tok)[:, None] < real[0], upstream[0], 0)
    both = jnp.concatenate([inputs[0], ahead.astype(bf16)], axis=0)
    xs = []
    for r in range(nx):
        piece = lax.dynamic_slice_in_dim(both, (c ^ r) * hw, hw, axis=1)
        xs.append(over_context(after(piece, gate), r) if r else piece)

    own = jnp.concatenate([proj_weight, delta_weight], axis=0)
    moves = [(a * nt + k, (k * groups + a % groups) * nt + a // groups) for a in range(m) for k in range(nt)]
    own = lax.ppermute(after(own, gate), plane + ("tensor",), moves)

    projected = token_sum([pieces[0]] + [over_context(pieces[k], k) for k in range(1, nx)], real)
    mixed = [projected] + [over_context(projected, k) for k in range(1, nx)]

    starts = jnp.cumsum(doc_lengths[0]) - doc_lengths[0]
    info = jnp.concatenate([jnp.reshape(c, (1,)), starts]).astype(jnp.int32)
    own = after(own, mixed[nx - 1], xs[nx - 1])
    value_parts, grad_parts = ssd(info, decay_rate[:, None], step_bias[:, None], xs, mixed, ndoc)

    height = own.shape[0]
    if nx == 4:
        one, two = over_context(own, 1), over_context(own, 2)
        one_late, two_late = after((one, two), grad_parts[0])
        cut = height // 2
        three = (over_context(one_late[:cut], 2), over_context(two_late[cut:], 1))
        weights = [(own,), (one,), (two,), three]
    else:
        weights = [(own,)] + [(over_context(own, k),) for k in range(1, nx)]
    for r in range(1, nd):
        weights += [tuple(over_dp(a, r) for a in piece) for piece in weights[:nx]]

    wr = gradient_sum([grad_parts[0]] + [over_context(grad_parts[k], k) for k in range(1, nx)], real)
    wr_groups = [wr] + [over_tensor(wr, k) for k in range(1, nt)]
    wr_all = [wr] + [over_context(wr, k) for k in range(1, nx)]
    stacked = jnp.stack(wr_all)
    for r in range(1, nd):
        other = over_dp(stacked, r)
        wr_all += [other[k] for k in range(nx)]
    proj_update, delta_update, sums = update(wr_all, columns, (proj_moment, proj_second, delta_moment, delta_second), nd)

    back = [value_parts[0]] + [over_context(value_parts[k], k) for k in range(1, nx)]
    place = jnp.stack([p, t, c]).astype(jnp.int32)
    hidden_grad, input_grad = hidden_gradient(place, wr_groups, back, weights, groups)
    return input_grad[None], hidden_grad[None], sums[:, 0], sums[:, 1], proj_update, delta_update


def solution(mesh):
    whole = ("dp", "context")
    return jax.shard_map(
        shards,
        mesh=mesh,
        in_specs=(
            P("dp", "context", None), P("dp", "context", "tensor"), P("dp", "context", "tensor"),
            P("tensor", whole), P("tensor", whole), P("tensor"), P("tensor"),
            P("tensor", whole), P("tensor", whole), P("tensor", whole), P("tensor", whole),
            P("dp", None), P("dp", "context"),
        ),
        out_specs=(
            P("dp", "context", "tensor"), P("dp", "context", "tensor"), P("tensor"), P("tensor"),
            P("tensor", whole), P("tensor", whole),
        ),
        check_vma=False,
    )
```
